32 devices in a mesh: hi: 4 (over x, core), lo: 8 (over z, y).
Axes of the slice: x: 2, y: 2, z: 4, core: 2. Of those that a mesh axis runs over, the one named last changes fastest.
Arguments:
- queries: bfloat16 [4096, 512], P(('hi', 'lo')), may hold values from -50 to 50
- key_rows: bfloat16 [4096, 128], P(('hi', 'lo')), may hold values from -6 to 6
- value_rows: bfloat16 [4096, 128], P(('hi', 'lo')), may hold values from -6 to 6
- global_positions: int32 [32, 8], P(('hi', 'lo')), may hold values from 0 to 127, as said below
Outputs:
- attended: bfloat16 [4096, 512], P(('hi', 'lo'))
The draws below stay inside these ranges and needn't reach their ends.
Inputs may be any that keep to these rules, and one draw needn't show every extreme that they name: `global_positions`: each row holds 8 distinct positions within a block.
All inputs are finite; a program needn't handle non-finite values.
Results may differ from the reference program's by a relative error of at most 0.0045.
Values may be sent and summed in bfloat16 or wider, within the bound.
A program may use at most 64 MiB of HBM per device.

```python
import jax
import jax.numpy as jnp
from jax import lax

H = 4
HD = 128
GLOB = 8
BLK = 128
NBLK = 32
TOKENS = 4096
N_HI = 4
N_LO = 8


def draw_key_rows(key, part):
    base = jax.random.fold_in(key, 11)
    rows = jnp.clip(jax.random.normal(base, (TOKENS, HD), jnp.float32), -6.0, 6.0)
    return rows.astype(jnp.bfloat16)


def draw_queries(key, part):
    base = jax.random.fold_in(key, 23)
    rows = 2.5 * jnp.clip(jax.random.normal(base, (TOKENS, H * HD), jnp.float32), -6.0, 6.0)
    return rows.astype(jnp.bfloat16)


def pick_slots(block_key):
    return jax.random.permutation(block_key, BLK)[:GLOB]


def draw_global_positions(key, part):
    base = jax.random.fold_in(key, 31)
    block_keys = jax.random.split(base, NBLK)
    return jax.vmap(pick_slots)(block_keys).astype(jnp.int32)


def shard_levels(own_key, shape, pieces, low, high):
    def one(position, parts):
        steps = jax.random.uniform(jax.random.fold_in(jax.random.fold_in(own_key, 6), position), (parts,), jnp.float32, low / len(pieces), high / len(pieces))
        return jnp.repeat(jnp.exp(steps), shape[position] // parts).reshape((-1,) + (1,) * (len(shape) - position - 1))

    loudness = one(*pieces[0])
    for cut in pieces[1:]:
        loudness = loudness * one(*cut)
    return loudness


def centred(rng, dims, deviation, bound, shards=(), kind=jnp.bfloat16):
    drawn = deviation * jax.random.normal(rng, dims, jnp.float32)
    if shards:
        drawn = drawn * shard_levels(rng, dims, shards, -0.22, 0.18)
    return jnp.clip(drawn, -bound, bound).astype(kind)


def setup_inputs(seed: int = 0) -> dict:
    seeds = jax.random.split(jax.random.key(seed), 5)
    queries = draw_queries(jax.random.fold_in(seeds[4], 71), 0)
    key_rows = draw_key_rows(jax.random.fold_in(seeds[4], 71), 0)
    value_rows = centred(seeds[2], (TOKENS, HD), 1.0, 6.0, ((0, 32),))
    global_positions = draw_global_positions(jax.random.fold_in(seeds[4], 71), 0)
    return {"queries": queries, "key_rows": key_rows, "value_rows": value_rows, "global_positions": global_positions}


def reference(queries, key_rows, value_rows, global_positions):
    block_count = N_HI * N_LO
    bit_count = block_count.bit_length() - 1
    starts = jnp.arange(block_count, dtype=jnp.int32)[:, None] * BLK
    flat_rows = (starts + global_positions.astype(jnp.int32)).reshape(-1)
    global_keys = jnp.take(key_rows, flat_rows, axis=0).astype(jnp.float32)
    global_values = jnp.take(value_rows, flat_rows, axis=0).astype(jnp.float32)
    blocked_keys = key_rows.reshape(block_count, BLK, HD).astype(jnp.float32)
    blocked_values = value_rows.reshape(block_count, BLK, HD).astype(jnp.float32)
    blocked_queries = queries.reshape(block_count, BLK, H, HD).astype(jnp.float32)

    def one_block(block_index):
        partner_list = [block_index] + [jnp.bitwise_xor(block_index, jnp.int32(1 << j)) for j in range(bit_count)]
        all_keys = jnp.concatenate([blocked_keys[p] for p in partner_list] + [global_keys], axis=0)
        all_values = jnp.concatenate([blocked_values[p] for p in partner_list] + [global_values], axis=0)
        scores = jnp.einsum("qhd,kd->hqk", blocked_queries[block_index], all_keys, precision=lax.Precision.HIGHEST) * (HD ** -0.5)
        row_peak = jnp.max(scores, axis=2, keepdims=True)
        raw_weights = jnp.exp(scores - row_peak)
        denominator = jnp.sum(raw_weights, axis=2)
        weights = lax.optimization_barrier(raw_weights.astype(jnp.bfloat16)).astype(jnp.float32)
        numerator = jnp.einsum("hqk,kd->qhd", weights, all_values, precision=lax.Precision.HIGHEST)
        result = numerator / jnp.transpose(denominator)[:, :, None]
        return result.reshape(BLK, H * HD).astype(jnp.bfloat16)

    attended = lax.map(one_block, jnp.arange(block_count, dtype=jnp.int32))
    return attended.reshape(TOKENS, H * HD)
```

```python
import functools
import math

import jax
import jax.numpy as jnp
from jax import lax
from jax.experimental import pallas as pl
from jax.experimental.pallas import tpu as pltpu
from jax.sharding import PartitionSpec as P

MESH = pl.DeviceIdType.MESH
GROUP_ROWS = 512


def dot(a, b, dims):
    return lax.dot_general(a, b, (dims, ((), ())), preferred_element_type=jnp.float32)


def attend(state, stacked, keys, values, factor):
    scores = dot(keys, stacked, ((1,), (1,)))
    fresh = jnp.max(scores, axis=0, keepdims=True)
    if state is not None:
        running, denominator, numerator = state
        fresh = jnp.maximum(running, fresh)
    weights = jnp.exp2((scores - fresh) * factor)
    total = jnp.sum(weights, axis=0, keepdims=True)
    update = dot(values, weights.astype(jnp.bfloat16), ((0,), (0,)))
    if state is not None:
        fade = jnp.exp2((running - fresh) * factor)
        total = denominator * fade + total
        update = numerator * fade + update
    return fresh, total, update


def flipped(index, mask):
    bit = 1
    while bit <= mask:
        if mask & bit:
            index = index + bit - 2 * bit * lax.rem(lax.div(index, bit), 2)
        bit *= 2
    return index


def kernel(
    n_hi, n_lo, q_hbm, k_hbm, v_hbm, pos_hbm, out_ref,
    q, k, v, pos, slabs, k_in, v_in,
    local_sem, ready, far_send, far_recv, near_send, near_recv, direct_send, block_send, block_recv,
):
    hi, lo = lax.axis_index("hi"), lax.axis_index("lo")
    barrier = pltpu.get_barrier_semaphore()
    n_far, n_near, total = n_lo // 2, n_hi * 2, n_hi * n_lo
    level = lax.div(lo, 2)

    def rank(h, l):
        distance = lax.div(h, 2) + lax.div(l, 2) + lax.rem(l, 2)
        return distance * total + h * n_lo + l

    def peer_of(f, e):
        h, l = flipped(hi, e // 2), flipped(lo, 2 * f + e % 2)
        return {"hi": h, "lo": l}, rank(h, l) < rank(hi, lo)

    near = {e: peer_of(0, e) for e in range(1, n_near)}
    far = {f: peer_of(f, 0) for f in range(1, n_far)}
    slot = {("near", e): e - 1 for e in near} | {("far", f): n_near - 2 + f for f in far}
    peers = {("near", e): p for e, p in near.items()} | {("far", f): p for f, p in far.items()}

    fetches = [
        pltpu.make_async_copy(source, target, local_sem.at[i])
        for i, (source, target) in enumerate(
            [(pos_hbm, pos), (k_hbm, k), (v_hbm, v), (q_hbm, q)]
        )
    ]
    for fetch in fetches:
        fetch.start()

    for peer, inner in peers.values():
        @pl.when(jnp.logical_not(inner))
        def _():
            pl.semaphore_signal(barrier, inc=1, device_id=peer, device_id_type=MESH)

    first_chip = jnp.logical_and(hi < 2, lo == 0)
    column = jnp.logical_and(hi < 2, lax.rem(lo, 2) == 0)

    @pl.when(first_chip)
    def _():
        def greet(i, carry):
            h, l = lax.rem(i, n_hi), 2 + lax.div(i, n_hi)

            @pl.when(jnp.logical_or(h != hi, lax.rem(l, 2) == 1))
            def _():
                pl.semaphore_signal(barrier, inc=1, device_id={"hi": h, "lo": l}, device_id_type=MESH)

            return carry

        lax.fori_loop(0, n_hi * (n_lo - 2), greet, 0)

    heard = sum(inner.astype(jnp.int32) for _, inner in peers.values())
    heard = heard + jnp.where(level > 0, 2 - column.astype(jnp.int32), 0)

    @pl.when(heard > 0)
    def _():
        pl.semaphore_wait(barrier, heard)

    for key, (peer, inner) in peers.items():
        @pl.when(inner)
        def _():
            pl.semaphore_signal(ready.at[slot[key]], inc=1, device_id=peer, device_id_type=MESH)

    for fetch in fetches[:3]:
        fetch.wait()

    block_rows, width = k.shape
    heads = q.shape[1] // width
    glob = pos.shape[1]
    factor = width**-0.5 * math.log2(math.e)

    row = lax.broadcasted_iota(jnp.int32, (2 * glob, block_rows), 0)
    column_of = lax.broadcasted_iota(jnp.int32, (2 * glob, block_rows), 1)
    wanted = jnp.zeros_like(row)
    for i in range(glob):
        wanted = jnp.where(lax.rem(row, glob) == i, pos[0, i], wanted)
    one_hot = jnp.where(column_of == wanted, 1.0, 0.0).astype(jnp.bfloat16)
    picked_k = dot(one_hot, k[...], ((1,), (0,)))
    picked_v = dot(one_hot, v[...], ((1,), (0,)))
    top = lax.broadcasted_iota(jnp.int32, picked_k.shape, 0) < glob
    slabs[0, 0] = jnp.where(top, picked_k, picked_v).astype(jnp.bfloat16)

    directs = []
    for c in range(2):
        e = 2 * (hi + c - 2 * c * lax.rem(hi, 2)) + lax.rem(lo, 2)
        directs.append((
            jnp.logical_and(level > 0, e > 0),
            pltpu.make_async_remote_copy(
                slabs.at[0, 0], slabs.at[e, level], direct_send.at[c], near_recv.at[level],
                device_id={"hi": c, "lo": 0}, device_id_type=MESH,
            ),
        ))
    for wanted_there, copy in directs:
        pl.when(wanted_there)(copy.start)

    far_copies = {
        f: pltpu.make_async_remote_copy(
            slabs.at[0, 0], slabs.at[0, f], far_send.at[f], far_recv.at[f],
            device_id=far[f][0], device_id_type=MESH,
        )
        for f in far
    }

    def near_copy(e, f):
        return pltpu.make_async_remote_copy(
            slabs.at[0, f], slabs.at[e, f], near_send.at[e, f], near_recv.at[f],
            device_id=near[e][0], device_id_type=MESH,
        )

    lo_bits, hi_bits = n_lo.bit_length() - 1, n_hi.bit_length() - 1
    partners = [("near", 2 * 2**b) for b in range(hi_bits)] + [("near", 1)] + [("far", 2**b) for b in range(lo_bits - 1)]
    blocks = {
        key: [
            pltpu.make_async_remote_copy(
                source, place.at[j], block_send.at[i, j], block_recv.at[i, j],
                device_id=peers[key][0], device_id_type=MESH,
            )
            for i, (source, place) in enumerate([(k, k_in), (v, v_in)])
        ]
        for j, key in enumerate(partners)
    }
    order = [("far", f) for f in reversed(far)] + [("near", e) for e in reversed(near)]

    def slab_start(key):
        (far_copies[key[1]] if key[0] == "far" else near_copy(key[1], 0)).start()

    def block_start(key):
        for copy in blocks.get(key, ()):
            copy.start()

    for key in order:
        pl.when(peers[key][1])(functools.partial(slab_start, key))
    for key in order:
        if key in blocks:
            pl.when(peers[key][1])(functools.partial(block_start, key))

    fetches[3].wait()
    stacked = jnp.concatenate([q[:, h * width : (h + 1) * width] for h in range(heads)], axis=0)
    state = attend(None, stacked, k[...], v[...], factor)

    outward = [("near", e) for e in near] + [("far", f) for f in far]
    for key in outward:
        @pl.when(jnp.logical_not(peers[key][1]))
        def _():
            pl.semaphore_wait(ready.at[slot[key]], 1)
            slab_start(key)
    for key in outward:
        if key in blocks:
            pl.when(jnp.logical_not(peers[key][1]))(functools.partial(block_start, key))

    def relayed(e):
        target = near[e][0]
        return jnp.logical_not(jnp.logical_and(target["hi"] < 2, target["lo"] == 0))

    for f in far:
        far_copies[f].wait_recv()
        for e in reversed(near):
            pl.when(relayed(e))(near_copy(e, f).start)

    for copies in blocks.values():
        for copy in copies:
            copy.wait_recv()
    rows = len(partners) * block_rows
    state = attend(
        state, stacked, k_in[...].reshape(rows, width), v_in[...].reshape(rows, width), factor
    )

    group = max(1, GROUP_ROWS // (n_near * glob))
    cuts = list(range(0, n_far - 1, group)) + [n_far - 1, n_far]
    for begin, end in zip(cuts, cuts[1:]):
        for f in range(begin, end):
            pltpu.make_async_copy(slabs.at[1:, f], slabs.at[1:, f], near_recv.at[f]).wait()
        mixed = slabs[:, begin:end].astype(jnp.float32)
        rows = (end - begin) * n_near * glob
        keys = mixed[:, :, :glob].reshape(rows, width).astype(jnp.bfloat16)
        values = mixed[:, :, glob:].reshape(rows, width).astype(jnp.bfloat16)
        state = attend(state, stacked, keys, values, factor)

    _, denominator, numerator = state
    result = numerator * (1.0 / denominator)
    for h in range(heads):
        part = result[:, h * block_rows : (h + 1) * block_rows]
        out_ref[:, h * width : (h + 1) * width] = jnp.transpose(part).astype(out_ref.dtype)

    for copy in far_copies.values():
        copy.wait_send()
    for copies in blocks.values():
        for copy in copies:
            copy.wait_send()
    for wanted_there, copy in directs:
        pl.when(wanted_there)(copy.wait_send)
    for e in near:
        near_copy(e, 0).wait_send()

        @pl.when(relayed(e))
        def _():
            for f in far:
                near_copy(e, f).wait_send()


def local(n_hi, n_lo, queries, key_rows, value_rows, global_positions):
    partners = (n_lo.bit_length() - 1) + (n_hi.bit_length() - 1)
    glob = global_positions.shape[1]
    width = key_rows.shape[1]
    dma = pltpu.SemaphoreType.DMA
    return pl.pallas_call(
        functools.partial(kernel, n_hi, n_lo),
        out_shape=jax.ShapeDtypeStruct(queries.shape, queries.dtype),
        in_specs=[pl.BlockSpec(memory_space=pltpu.HBM)] * 4,
        out_specs=pl.BlockSpec(memory_space=pltpu.VMEM),
        scratch_shapes=[
            pltpu.VMEM(queries.shape, queries.dtype),
            pltpu.VMEM(key_rows.shape, key_rows.dtype),
            pltpu.VMEM(value_rows.shape, value_rows.dtype),
            pltpu.SMEM(global_positions.shape, global_positions.dtype),
            pltpu.VMEM((2 * n_hi, n_lo // 2, 2 * glob, width), key_rows.dtype),
            pltpu.VMEM((partners,) + key_rows.shape, key_rows.dtype),
            pltpu.VMEM((partners,) + value_rows.shape, value_rows.dtype),
            dma((4,)),
            pltpu.SemaphoreType.REGULAR((n_lo // 2 + 2 * n_hi - 2,)),
            dma((n_lo // 2,)),
            dma((n_lo // 2,)),
            dma((2 * n_hi, n_lo // 2)),
            dma((n_lo // 2,)),
            dma((2,)),
            dma((2, partners)),
            dma((2, partners)),
        ],
        compiler_params=pltpu.CompilerParams(collective_id=0, has_side_effects=True, vmem_limit_bytes=12 * 2**20),
    )(*(pltpu.with_memory_space_constraint(x, pltpu.HBM) for x in (queries, key_rows, value_rows, global_positions)))


def solution(mesh):
    spec = P(("hi", "lo"), None)
    return jax.shard_map(
        functools.partial(local, mesh.shape["hi"], mesh.shape["lo"]),
        mesh=mesh,
        in_specs=(spec,) * 4,
        out_specs=spec,
        check_vma=False,
    )
```

```python
import functools
import math

import jax
import jax.numpy as jnp
from jax import lax
from jax.experimental import pallas as pl
from jax.experimental.pallas import tpu as pltpu
from jax.sharding import PartitionSpec as P

MESH = pl.DeviceIdType.MESH
DIRECT = [(0, 0), (1, 0)]
CARRY = True
LIFT = False


def dot(a, b, dims):
    return lax.dot_general(a, b, (dims, ((), ())), preferred_element_type=jnp.float32)


def attend(state, stacked, keys, values, factor):
    scores = dot(keys, stacked, ((1,), (1,)))
    fresh = jnp.max(scores, axis=0, keepdims=True)
    if state is not None:
        running, denominator, numerator = state
        fresh = jnp.maximum(running, fresh)
    weights = jnp.exp2((scores - fresh) * factor)
    total = jnp.sum(weights, axis=0, keepdims=True)
    update = dot(values, weights.astype(jnp.bfloat16), ((0,), (0,)))
    if state is not None:
        fade = jnp.exp2((running - fresh) * factor)
        total = denominator * fade + total
        update = numerator * fade + update
    return fresh, total, update


def turns(index, size):
    bits = (2**b for b in range(size.bit_length() - 1))
    return [1 - 2 * lax.rem(lax.div(index, bit), 2) for bit in bits]


def change(signs, mask, weight=lambda b: 2**b):
    parts = [sign * weight(b) for b, sign in enumerate(signs) if mask & 2**b and weight(b)]
    return sum(parts[1:], parts[0]) if parts else 0


def count(flags):
    return sum(flag.astype(jnp.int32) for flag in flags)


def kernel(
    n_hi, n_lo, q_hbm, k_hbm, v_hbm, pos_hbm, out_ref,
    q, kv, pos, slabs, kv_in, local_sem, ready, far_recv, rest_recv, send, block_recv,
):
    fetch_pos = pltpu.make_async_copy(pos_hbm, pos, local_sem.at[0])
    fetch_q = pltpu.make_async_copy(q_hbm, q, local_sem.at[2])
    fetch_pos.start()
    pltpu.make_async_copy(k_hbm, kv.at[0], local_sem.at[1]).start()
    pltpu.make_async_copy(v_hbm, kv.at[1], local_sem.at[1]).start()
    fetch_q.start()

    hi, lo = lax.axis_index("hi"), lax.axis_index("lo")
    barrier = pltpu.get_barrier_semaphore()
    n_far, n_near, total = n_lo // 2, n_hi * 2, n_hi * n_lo
    level, side = lax.div(lo, 2), lax.rem(lo, 2)
    across = lax.div(hi, 2) + side
    top = level == n_far - 1
    hi_signs, lo_signs = turns(hi, n_hi), turns(lo, n_lo)

    def outward(mask_hi, mask_lo):
        return change(hi_signs, mask_hi, lambda b: 2**b // 2) + change(lo_signs, mask_lo, lambda b: max(1, 2**b // 2))

    def peer_of(f, e):
        mask_hi, mask_lo = e // 2, 2 * f + e % 2
        up, along = change(hi_signs, mask_hi), change(lo_signs, mask_lo)
        inner = outward(mask_hi, mask_lo) * total + up * n_lo + along < 0
        return {"hi": hi + up, "lo": lo + along}, inner

    near = {e: peer_of(0, e) for e in range(1, n_near)}
    far = {f: peer_of(f, 0) for f in range(1, n_far)}
    peers = {("near", e): p for e, p in near.items()} | {("far", f): p for f, p in far.items()}
    near_keys, far_keys = [("near", e) for e in near], [("far", f) for f in far]

    def signal(semaphore, device):
        pl.semaphore_signal(semaphore, inc=1, device_id=device, device_id_type=MESH)

    for peer, inner in peers.values():
        pl.when(jnp.logical_not(inner))(functools.partial(signal, barrier, peer))

    @pl.when(jnp.logical_and(level == 0, across == 0))
    def _():
        def greet(i, carry):
            h, l = lax.rem(i, n_hi), 2 + lax.div(i, n_hi)

            @pl.when(jnp.logical_or(h != hi, lax.rem(l, 2) == 1))
            def _():
                signal(barrier, {"hi": h, "lo": l})

            return carry

        lax.fori_loop(0, n_hi * (n_lo - 2), greet, 0)

    heard = count(inner for _, inner in peers.values())
    heard = heard + jnp.where(level > 0, 2 - (across == 0).astype(jnp.int32), 0)

    @pl.when(heard > 0)
    def _():
        pl.semaphore_wait(barrier, heard)

    for (kind, index), (peer, inner) in peers.items():
        pl.when(inner)(functools.partial(signal, ready.at[0 if kind == "near" else index], peer))

    fetch_pos.wait()
    pltpu.make_async_copy(kv, kv, local_sem.at[1]).wait()
    block_rows, width = k_hbm.shape
    heads = q.shape[1] // width
    glob = pos.shape[1]
    factor = width**-0.5 * math.log2(math.e)

    row = lax.broadcasted_iota(jnp.int32, (2 * glob, block_rows), 0)
    column = lax.broadcasted_iota(jnp.int32, (2 * glob, block_rows), 1)
    wanted = jnp.zeros_like(row)
    for i in range(glob):
        wanted = jnp.where(lax.rem(row, glob) == i, pos[0, i], wanted)
    one_hot = jnp.where(column == wanted, 1.0, 0.0).astype(jnp.bfloat16)
    picked_k = dot(one_hot, kv[0], ((1,), (0,)))
    picked_v = dot(one_hot, kv[1], ((1,), (0,)))
    upper = lax.broadcasted_iota(jnp.int32, picked_k.shape, 0) < glob
    slabs[0, 0] = jnp.where(upper, picked_k, picked_v).astype(jnp.bfloat16)

    def slab_copy(e, f, semaphore, device, source=(0, 0)):
        return pltpu.make_async_remote_copy(
            slabs.at[source], slabs.at[e, f], send.at[0], semaphore,
            device_id=device, device_id_type=MESH,
        )

    directs = []
    for h, l in DIRECT:
        e = 2 * (hi + change(hi_signs, h)) + (1 - side if l else side)
        wanted_there = jnp.logical_and(level > 0 if h < 2 and l == 0 else top, e > 0)
        pl.when(wanted_there)(slab_copy(e, level, rest_recv, {"hi": h, "lo": l}).start)
        directs.append(wanted_there)

    lo_bits, hi_bits = n_lo.bit_length() - 1, n_hi.bit_length() - 1
    near_partners = [("near", 2 * 2**b) for b in range(hi_bits)] + [("near", 1)]
    far_partners = [("far", 2**b) for b in range(lo_bits - 1)]
    partners = near_partners + far_partners

    def slab_start(key):
        kind, index = key
        if kind == "near":
            slab_copy(index, 0, far_recv.at[0], near[index][0]).start()
        else:
            slab_copy(0, index, far_recv.at[index], far[index][0]).start()

    def block_start(key):
        pltpu.make_async_remote_copy(
            kv, kv_in.at[partners.index(key)], send.at[1],
            block_recv.at[0 if key in near_partners else 1],
            device_id=peers[key][0], device_id_type=MESH,
        ).start()

    inward = list(reversed(far_keys)) + list(reversed(near_keys))
    for key in inward:
        pl.when(peers[key][1])(functools.partial(slab_start, key))
    for key in inward:
        if key in partners:
            pl.when(peers[key][1])(functools.partial(block_start, key))

    fetch_q.wait()
    stacked = jnp.concatenate([q[:, h * width : (h + 1) * width] for h in range(heads)], axis=0)
    state = attend(None, stacked, kv[0], kv[1], factor)

    def outer(key, action):
        pl.when(jnp.logical_not(peers[key][1]))(functools.partial(action, key))

    def answered(key):
        pl.semaphore_wait(ready.at[key[1]], 1)
        slab_start(key)

    outer_near = n_near - 1 - count(inner for _, inner in near.values())

    def outward_near():
        @pl.when(outer_near > 0)
        def _():
            pl.semaphore_wait(ready.at[0], outer_near)

        for key in near_keys:
            outer(key, slab_start)
        for key in near_partners:
            outer(key, block_start)

    def outward_far(slab_keys, block_keys):
        for key in slab_keys:
            outer(key, answered)
        for key in block_keys:
            if key in far_partners:
                outer(key, block_start)

    outward_far(far_keys[:1], far_keys[:1])
    outward_near()
    outward_far(far_keys[1:], far_keys[1:])

    climb = n_far - 1 - level
    spread = {e: outward(e // 2, e % 2) for e in near}
    lower = {f: outward(0, 2 * f) < 0 for f in far}
    wide = [e for e in near if e // 4 and e % 2] if LIFT else []

    def served(e, f):
        target = near[e][0]
        flags = [jnp.logical_and(target["hi"] < 2, target["lo"] == 0)]
        if CARRY:
            limit = jnp.where(top, -1 if e == 2 else 0, -2 if e in wide else -total)
            flags.append(jnp.logical_and(lower[f], spread[e] <= limit))
        if f == n_far - 1 and len(DIRECT) > 2:
            flags.append(jnp.logical_and(level == 0, across + spread[e] <= 1))
        return functools.reduce(jnp.logical_or, flags)

    relays = {(e, f): jnp.logical_not(served(e, f)) for f in far for e in near}
    carried = {e: jnp.logical_and(jnp.logical_not(top), spread[e] >= (1 if e == 2 else 0)) for e in near} if CARRY else {}
    lifted = {}
    for f in far:
        beyond = jnp.logical_and(jnp.logical_not(lower[f]), climb != f)
        for e in wide:
            lifted[e, f] = jnp.logical_and(beyond, spread[e] >= 2)

    def relay(f):
        slab = slabs.at[0, f]
        pltpu.make_async_copy(slab, slab, far_recv.at[f]).wait()
        for e in reversed(near):
            pl.when(relays[e, f])(slab_copy(e, f, rest_recv, near[e][0], (0, f)).start)

    def raise_slabs():
        group = slabs.at[1:, 0]
        pltpu.make_async_copy(group, group, far_recv.at[0]).wait()
        for e, flag in carried.items():
            pl.when(flag)(slab_copy(e, climb, rest_recv, {"lo": lo + 2 * climb}, (e, 0)).start)
        for (e, f), flag in lifted.items():
            pl.when(flag)(slab_copy(e, f, rest_recv, far[f][0], (e, 0)).start)

    def take(state, begin, end, semaphore):
        group = kv_in.at[begin:end]
        pltpu.make_async_copy(group, group, semaphore).wait()
        rows = (end - begin) * block_rows
        keys = kv_in[begin:end, 0].reshape(rows, width)
        values = kv_in[begin:end, 1].reshape(rows, width)
        return attend(state, stacked, keys, values, factor)

    def gather(state, begin, end):
        mixed = slabs[:, begin:end].astype(jnp.float32)
        rows = (end - begin) * n_near * glob
        keys = mixed[:, :, :glob].reshape(rows, width).astype(jnp.bfloat16)
        values = mixed[:, :, glob:].reshape(rows, width).astype(jnp.bfloat16)
        return attend(state, stacked, keys, values, factor)

    for f in range(1, n_far - 1):
        relay(f)
    raise_slabs()
    relay(n_far - 1)
    state = take(state, 0, len(near_partners), block_recv.at[0])
    state = take(state, len(near_partners), len(partners), block_recv.at[1])
    state = gather(state, 0, 1)

    pltpu.make_async_copy(kv_in, kv_in, send.at[1]).wait()
    sent = n_near + n_far - 2 + count([*directs, *relays.values(), *carried.values(), *lifted.values()])
    amount = 1
    while amount <= total:
        part = slabs.at[0, :amount] if amount <= n_far else slabs.at[: amount // n_far]
        pl.when(lax.rem(lax.div(sent, amount), 2) == 1)(pltpu.make_async_copy(part, part, send.at[0]).wait)
        amount *= 2

    rest = slabs.at[1:, 1:]
    pltpu.make_async_copy(rest, rest, rest_recv).wait()
    _, denominator, numerator = gather(state, 1, n_far)
    result = numerator * (1.0 / denominator)
    for h in range(heads):
        part = result[:, h * block_rows : (h + 1) * block_rows]
        out_ref[:, h * width : (h + 1) * width] = jnp.transpose(part).astype(out_ref.dtype)


def local(n_hi, n_lo, queries, key_rows, value_rows, global_positions):
    partners = (n_lo.bit_length() - 1) + (n_hi.bit_length() - 1)
    glob = global_positions.shape[1]
    width = key_rows.shape[1]
    dma = pltpu.SemaphoreType.DMA
    return pl.pallas_call(
        functools.partial(kernel, n_hi, n_lo),
        out_shape=jax.ShapeDtypeStruct(queries.shape, queries.dtype),
        in_specs=[pl.BlockSpec(memory_space=pltpu.HBM)] * 4,
        out_specs=pl.BlockSpec(memory_space=pltpu.VMEM),
        scratch_shapes=[
            pltpu.VMEM(queries.shape, queries.dtype),
            pltpu.VMEM((2,) + key_rows.shape, key_rows.dtype),
            pltpu.SMEM(global_positions.shape, global_positions.dtype),
            pltpu.VMEM((2 * n_hi, n_lo // 2, 2 * glob, width), key_rows.dtype),
            pltpu.VMEM((partners, 2) + key_rows.shape, key_rows.dtype),
            dma((3,)),
            pltpu.SemaphoreType.REGULAR((n_lo // 2,)),
            dma((n_lo // 2,)),
            dma,
            dma((2,)),
            dma((2,)),
        ],
        compiler_params=pltpu.CompilerParams(collective_id=0, has_side_effects=True, vmem_limit_bytes=12 * 2**20),
    )(*(pltpu.with_memory_space_constraint(x, pltpu.HBM) for x in (queries, key_rows, value_rows, global_positions)))


def solution(mesh):
    spec = P(("hi", "lo"), None)
    return jax.shard_map(
        functools.partial(local, mesh.shape["hi"], mesh.shape["lo"]),
        mesh=mesh,
        in_specs=(spec,) * 4,
        out_specs=spec,
        check_vma=False,
    )
```

```python
import functools
import math

import jax
import jax.numpy as jnp
from jax import lax
from jax.experimental import pallas as pl
from jax.experimental.pallas import tpu as pltpu
from jax.sharding import PartitionSpec as P

MESH = pl.DeviceIdType.MESH
DIRECT = [(0, 0), (1, 0), (0, 1), (1, 1), (2, 0), (3, 0)]
CARRY = True
LIFT = False


def dot(a, b, dims):
    return lax.dot_general(a, b, (dims, ((), ())), preferred_element_type=jnp.float32)


def attend(state, stacked, keys, values, factor):
    scores = dot(keys, stacked, ((1,), (1,)))
    fresh = jnp.max(scores, axis=0, keepdims=True)
    if state is not None:
        running, denominator, numerator = state
        fresh = jnp.maximum(running, fresh)
    weights = jnp.exp2((scores - fresh) * factor)
    total = jnp.sum(weights, axis=0, keepdims=True)
    update = dot(values, weights.astype(jnp.bfloat16), ((0,), (0,)))
    if state is not None:
        fade = jnp.exp2((running - fresh) * factor)
        total = denominator * fade + total
        update = numerator * fade + update
    return fresh, total, update


def turns(index, size):
    bits = (2**b for b in range(size.bit_length() - 1))
    return [1 - 2 * lax.rem(lax.div(index, bit), 2) for bit in bits]


def change(signs, mask, weight=lambda b: 2**b):
    parts = [sign * weight(b) for b, sign in enumerate(signs) if mask & 2**b and weight(b)]
    return sum(parts[1:], parts[0]) if parts else 0


def count(flags):
    return sum(flag.astype(jnp.int32) for flag in flags)


def kernel(
    n_hi, n_lo, q_hbm, k_hbm, v_hbm, pos_hbm, out_ref,
    q, kv, pos, slabs, kv_in, local_sem, ready, far_recv, rest_recv, send, block_recv,
):
    fetch_pos = pltpu.make_async_copy(pos_hbm, pos, local_sem.at[0])
    fetch_q = pltpu.make_async_copy(q_hbm, q, local_sem.at[2])
    fetch_pos.start()
    pltpu.make_async_copy(k_hbm, kv.at[0], local_sem.at[1]).start()
    pltpu.make_async_copy(v_hbm, kv.at[1], local_sem.at[1]).start()
    fetch_q.start()

    hi, lo = lax.axis_index("hi"), lax.axis_index("lo")
    barrier = pltpu.get_barrier_semaphore()
    n_far, n_near, total = n_lo // 2, n_hi * 2, n_hi * n_lo
    level, side = lax.div(lo, 2), lax.rem(lo, 2)
    across = lax.div(hi, 2) + side
    top = level == n_far - 1
    hi_signs, lo_signs = turns(hi, n_hi), turns(lo, n_lo)

    def outward(mask_hi, mask_lo):
        return change(hi_signs, mask_hi, lambda b: 2**b // 2) + change(lo_signs, mask_lo, lambda b: max(1, 2**b // 2))

    def peer_of(f, e):
        mask_hi, mask_lo = e // 2, 2 * f + e % 2
        up, along = change(hi_signs, mask_hi), change(lo_signs, mask_lo)
        inner = outward(mask_hi, mask_lo) * total + up * n_lo + along < 0
        return {"hi": hi + up, "lo": lo + along}, inner

    near = {e: peer_of(0, e) for e in range(1, n_near)}
    far = {f: peer_of(f, 0) for f in range(1, n_far)}
    peers = {("near", e): p for e, p in near.items()} | {("far", f): p for f, p in far.items()}
    near_keys, far_keys = [("near", e) for e in near], [("far", f) for f in far]

    def signal(semaphore, device):
        pl.semaphore_signal(semaphore, inc=1, device_id=device, device_id_type=MESH)

    @pl.when(jnp.logical_and(level == 0, across == 1))
    def _():
        for h in range(n_hi):
            for y in range(2):
                if h > 1 or y:
                    flag = jnp.logical_or(h != hi, y != side)
                    pl.when(flag)(functools.partial(signal, barrier, {"hi": h, "lo": n_lo - 2 + y}))

    for peer, inner in peers.values():
        pl.when(jnp.logical_not(inner))(functools.partial(signal, barrier, peer))

    @pl.when(jnp.logical_and(level == 0, across == 0))
    def _():
        def greet(i, carry):
            h, l = lax.rem(i, n_hi), 2 + lax.div(i, n_hi)

            @pl.when(jnp.logical_or(h != hi, lax.rem(l, 2) == 1))
            def _():
                signal(barrier, {"hi": h, "lo": l})

            return carry

        lax.fori_loop(0, n_hi * (n_lo - 2), greet, 0)

    heard = count(inner for _, inner in peers.values())
    heard = heard + jnp.where(level > 0, 2 - (across == 0).astype(jnp.int32), 0)
    heard = heard + jnp.where(jnp.logical_and(top, across > 0), 4 - (across == 1).astype(jnp.int32), 0)

    @pl.when(heard > 0)
    def _():
        pl.semaphore_wait(barrier, heard)

    for (kind, index), (peer, inner) in peers.items():
        pl.when(inner)(functools.partial(signal, ready.at[0 if kind == "near" else index], peer))

    fetch_pos.wait()
    pltpu.make_async_copy(kv, kv, local_sem.at[1]).wait()
    block_rows, width = k_hbm.shape
    heads = q.shape[1] // width
    glob = pos.shape[1]
    factor = width**-0.5 * math.log2(math.e)

    row = lax.broadcasted_iota(jnp.int32, (2 * glob, block_rows), 0)
    column = lax.broadcasted_iota(jnp.int32, (2 * glob, block_rows), 1)
    wanted = jnp.zeros_like(row)
    for i in range(glob):
        wanted = jnp.where(lax.rem(row, glob) == i, pos[0, i], wanted)
    one_hot = jnp.where(column == wanted, 1.0, 0.0).astype(jnp.bfloat16)
    picked_k = dot(one_hot, kv[0], ((1,), (0,)))
    picked_v = dot(one_hot, kv[1], ((1,), (0,)))
    upper = lax.broadcasted_iota(jnp.int32, picked_k.shape, 0) < glob
    slabs[0, 0] = jnp.where(upper, picked_k, picked_v).astype(jnp.bfloat16)

    def slab_copy(e, f, semaphore, device, source=(0, 0)):
        return pltpu.make_async_remote_copy(
            slabs.at[source], slabs.at[e, f], send.at[0], semaphore,
            device_id=device, device_id_type=MESH,
        )

    directs = []

    def direct(targets):
        for h, l in targets:
            e = 2 * (hi + change(hi_signs, h)) + (1 - side if l else side)
            wanted_there = level > 0 if h < 2 and l == 0 else jnp.logical_and(top, across > 0)
            wanted_there = jnp.logical_and(wanted_there, e > 0)
            pl.when(wanted_there)(slab_copy(e, level, rest_recv, {"hi": h, "lo": l}).start)
            directs.append(wanted_there)

    direct(DIRECT[:2])

    lo_bits, hi_bits = n_lo.bit_length() - 1, n_hi.bit_length() - 1
    near_partners = [("near", 2 * 2**b) for b in range(hi_bits)] + [("near", 1)]
    far_partners = [("far", 2**b) for b in range(lo_bits - 1)]
    partners = near_partners + far_partners

    def slab_start(key):
        kind, index = key
        if kind == "near":
            slab_copy(index, 0, far_recv.at[0], near[index][0]).start()
        else:
            slab_copy(0, index, far_recv.at[index], far[index][0]).start()

    def block_start(key):
        pltpu.make_async_remote_copy(
            kv, kv_in.at[partners.index(key)], send.at[1],
            block_recv.at[0 if key in near_partners else 1],
            device_id=peers[key][0], device_id_type=MESH,
        ).start()

    inward = list(reversed(far_keys)) + list(reversed(near_keys))
    for key in inward:
        pl.when(peers[key][1])(functools.partial(slab_start, key))
    direct(DIRECT[2:])
    for key in inward:
        if key in partners:
            pl.when(peers[key][1])(functools.partial(block_start, key))

    fetch_q.wait()
    stacked = jnp.concatenate([q[:, h * width : (h + 1) * width] for h in range(heads)], axis=0)
    state = attend(None, stacked, kv[0], kv[1], factor)

    def outer(key, action):
        pl.when(jnp.logical_not(peers[key][1]))(functools.partial(action, key))

    def answered(key):
        pl.semaphore_wait(ready.at[key[1]], 1)
        slab_start(key)

    outer_near = n_near - 1 - count(inner for _, inner in near.values())

    def outward_near():
        @pl.when(outer_near > 0)
        def _():
            pl.semaphore_wait(ready.at[0], outer_near)

        for key in near_keys:
            outer(key, slab_start)
        for key in near_partners:
            outer(key, block_start)

    def outward_far(slab_keys, block_keys):
        for key in slab_keys:
            outer(key, answered)
        for key in block_keys:
            if key in far_partners:
                outer(key, block_start)

    outward_far(far_keys[:1], far_keys[:1])
    outward_near()
    outward_far(far_keys[1:], far_keys[1:])

    climb = n_far - 1 - level
    spread = {e: outward(e // 2, e % 2) for e in near}
    lower = {f: outward(0, 2 * f) < 0 for f in far}
    wide = [e for e in near if e // 4 and e % 2] if LIFT else []

    def served(e, f):
        target = near[e][0]
        flags = [jnp.logical_and(target["hi"] < 2, target["lo"] == 0)]
        if CARRY:
            limit = jnp.where(top, -1 if e == 2 else 0, -2 if e in wide else -total)
            flags.append(jnp.logical_and(lower[f], spread[e] <= limit))
        if f == n_far - 1 and len(DIRECT) > 2:
            edge = jnp.logical_and(level == 0, across > 0)
            flags.append(jnp.logical_and(edge, across + spread[e] <= 1))
        return functools.reduce(jnp.logical_or, flags)

    relays = {(e, f): jnp.logical_not(served(e, f)) for f in far for e in near}
    carried = {e: jnp.logical_and(jnp.logical_not(top), spread[e] >= (1 if e == 2 else 0)) for e in near} if CARRY else {}
    lifted = {}
    for f in far:
        beyond = jnp.logical_and(jnp.logical_not(lower[f]), climb != f)
        for e in wide:
            lifted[e, f] = jnp.logical_and(beyond, spread[e] >= 2)

    def relay(f):
        slab = slabs.at[0, f]
        pltpu.make_async_copy(slab, slab, far_recv.at[f]).wait()
        for e in reversed(near):
            pl.when(relays[e, f])(slab_copy(e, f, rest_recv, near[e][0], (0, f)).start)

    def raise_slabs():
        group = slabs.at[1:, 0]
        pltpu.make_async_copy(group, group, far_recv.at[0]).wait()
        for e, flag in carried.items():
            pl.when(flag)(slab_copy(e, climb, rest_recv, {"lo": lo + 2 * climb}, (e, 0)).start)
        for (e, f), flag in lifted.items():
            pl.when(flag)(slab_copy(e, f, rest_recv, far[f][0], (e, 0)).start)

    def take(state, begin, end, semaphore):
        group = kv_in.at[begin:end]
        pltpu.make_async_copy(group, group, semaphore).wait()
        rows = (end - begin) * block_rows
        keys = kv_in[begin:end, 0].reshape(rows, width)
        values = kv_in[begin:end, 1].reshape(rows, width)
        return attend(state, stacked, keys, values, factor)

    def gather(state, begin, end):
        mixed = slabs[:, begin:end].astype(jnp.float32)
        rows = (end - begin) * n_near * glob
        keys = mixed[:, :, :glob].reshape(rows, width).astype(jnp.bfloat16)
        values = mixed[:, :, glob:].reshape(rows, width).astype(jnp.bfloat16)
        return attend(state, stacked, keys, values, factor)

    for f in range(1, n_far - 1):
        relay(f)
    raise_slabs()
    relay(n_far - 1)
    state = take(state, 0, len(near_partners), block_recv.at[0])
    state = take(state, len(near_partners), len(partners), block_recv.at[1])
    state = gather(state, 0, 1)

    pltpu.make_async_copy(kv_in, kv_in, send.at[1]).wait()
    sent = n_near + n_far - 2 + count([*directs, *relays.values(), *carried.values(), *lifted.values()])
    amount = 1
    while amount <= total:
        part = slabs.at[0, :amount] if amount <= n_far else slabs.at[: amount // n_far]
        pl.when(lax.rem(lax.div(sent, amount), 2) == 1)(pltpu.make_async_copy(part, part, send.at[0]).wait)
        amount *= 2

    rest = slabs.at[1:, 1:]
    pltpu.make_async_copy(rest, rest, rest_recv).wait()
    _, denominator, numerator = gather(state, 1, n_far)
    result = numerator * (1.0 / denominator)
    for h in range(heads):
        part = result[:, h * block_rows : (h + 1) * block_rows]
        out_ref[:, h * width : (h + 1) * width] = jnp.transpose(part).astype(out_ref.dtype)


def local(n_hi, n_lo, queries, key_rows, value_rows, global_positions):
    partners = (n_lo.bit_length() - 1) + (n_hi.bit_length() - 1)
    glob = global_positions.shape[1]
    width = key_rows.shape[1]
    dma = pltpu.SemaphoreType.DMA
    return pl.pallas_call(
        functools.partial(kernel, n_hi, n_lo),
        out_shape=jax.ShapeDtypeStruct(queries.shape, queries.dtype),
        in_specs=[pl.BlockSpec(memory_space=pltpu.HBM)] * 4,
        out_specs=pl.BlockSpec(memory_space=pltpu.VMEM),
        scratch_shapes=[
            pltpu.VMEM(queries.shape, queries.dtype),
            pltpu.VMEM((2,) + key_rows.shape, key_rows.dtype),
            pltpu.SMEM(global_positions.shape, global_positions.dtype),
            pltpu.VMEM((2 * n_hi, n_lo // 2, 2 * glob, width), key_rows.dtype),
            pltpu.VMEM((partners, 2) + key_rows.shape, key_rows.dtype),
            dma((3,)),
            pltpu.SemaphoreType.REGULAR((n_lo // 2,)),
            dma((n_lo // 2,)),
            dma,
            dma((2,)),
            dma((2,)),
        ],
        compiler_params=pltpu.CompilerParams(collective_id=0, has_side_effects=True, vmem_limit_bytes=12 * 2**20),
    )(*(pltpu.with_memory_space_constraint(x, pltpu.HBM) for x in (queries, key_rows, value_rows, global_positions)))


def solution(mesh):
    spec = P(("hi", "lo"), None)
    return jax.shard_map(
        functools.partial(local, mesh.shape["hi"], mesh.shape["lo"]),
        mesh=mesh,
        in_specs=(spec,) * 4,
        out_specs=spec,
        check_vma=False,
    )
```

```python
import functools
import math

import jax
import jax.numpy as jnp
from jax import lax
from jax.experimental import pallas as pl
from jax.experimental.pallas import tpu as pltpu
from jax.sharding import PartitionSpec as P

MESH = pl.DeviceIdType.MESH
DIRECT = [(0, 0), (1, 0), (0, 1), (1, 1), (2, 0), (3, 0)]


def dot(a, b, dims):
    return lax.dot_general(a, b, (dims, ((), ())), preferred_element_type=jnp.float32)


def attend(state, stacked, keys, values, factor):
    scores = dot(keys, stacked, ((1,), (1,)))
    fresh = jnp.max(scores, axis=0, keepdims=True)
    if state is not None:
        running, denominator, numerator = state
        fresh = jnp.maximum(running, fresh)
    weights = jnp.exp2((scores - fresh) * factor)
    total = jnp.sum(weights, axis=0, keepdims=True)
    update = dot(values, weights.astype(jnp.bfloat16), ((0,), (0,)))
    if state is not None:
        fade = jnp.exp2((running - fresh) * factor)
        total = denominator * fade + total
        update = numerator * fade + update
    return fresh, total, update


def turns(index, size):
    bits = (2**b for b in range(size.bit_length() - 1))
    return [1 - 2 * lax.rem(lax.div(index, bit), 2) for bit in bits]


def change(signs, mask, weight=lambda b: 2**b):
    parts = [sign * weight(b) for b, sign in enumerate(signs) if mask & 2**b and weight(b)]
    return sum(parts[1:], parts[0]) if parts else 0


def count(flags):
    return sum(flag.astype(jnp.int32) for flag in flags)


def kernel(
    n_hi, n_lo, q_hbm, k_hbm, v_hbm, pos_hbm, out_ref,
    q, kv, pos, slabs, kv_in, local_sem, ready, far_recv, rest_recv, send, block_recv,
):
    fetch_pos = pltpu.make_async_copy(pos_hbm, pos, local_sem.at[0])
    fetch_q = pltpu.make_async_copy(q_hbm, q, local_sem.at[2])
    fetch_pos.start()
    pltpu.make_async_copy(k_hbm, kv.at[0], local_sem.at[1]).start()
    pltpu.make_async_copy(v_hbm, kv.at[1], local_sem.at[1]).start()
    fetch_q.start()

    hi, lo = lax.axis_index("hi"), lax.axis_index("lo")
    barrier = pltpu.get_barrier_semaphore()
    n_far, n_near, total = n_lo // 2, n_hi * 2, n_hi * n_lo
    level, side = lax.div(lo, 2), lax.rem(lo, 2)
    across = lax.div(hi, 2) + side
    top = level == n_far - 1
    hi_signs, lo_signs = turns(hi, n_hi), turns(lo, n_lo)

    def outward(mask_hi, mask_lo):
        return change(hi_signs, mask_hi, lambda b: 2**b // 2) + change(lo_signs, mask_lo, lambda b: max(1, 2**b // 2))

    def peer_of(f, e):
        mask_hi, mask_lo = e // 2, 2 * f + e % 2
        up, along = change(hi_signs, mask_hi), change(lo_signs, mask_lo)
        inner = outward(mask_hi, mask_lo) * total + up * n_lo + along < 0
        return {"hi": hi + up, "lo": lo + along}, inner

    near = {e: peer_of(0, e) for e in range(1, n_near)}
    far = {f: peer_of(f, 0) for f in range(1, n_far)}
    peers = {("near", e): p for e, p in near.items()} | {("far", f): p for f, p in far.items()}
    near_keys, far_keys = [("near", e) for e in near], [("far", f) for f in far]

    def signal(semaphore, device):
        pl.semaphore_signal(semaphore, inc=1, device_id=device, device_id_type=MESH)

    @pl.when(jnp.logical_and(level == 0, across == 1))
    def _():
        for h in range(n_hi):
            for y in range(2):
                if h > 1 or y:
                    flag = jnp.logical_or(h != hi, y != side)
                    pl.when(flag)(functools.partial(signal, barrier, {"hi": h, "lo": n_lo - 2 + y}))

    for peer, inner in peers.values():
        pl.when(jnp.logical_not(inner))(functools.partial(signal, barrier, peer))

    @pl.when(jnp.logical_and(level == 0, across == 0))
    def _():
        def greet(l, carry):
            for h in range(n_hi):
                pl.when(jnp.logical_or(h != hi, lax.rem(l, 2) == 1))(functools.partial(signal, barrier, {"hi": h, "lo": l}))
            return carry

        lax.fori_loop(2, n_lo, greet, 0)

    heard = count(inner for _, inner in peers.values())
    heard = heard + jnp.where(level > 0, 2 - (across == 0).astype(jnp.int32), 0)
    heard = heard + jnp.where(jnp.logical_and(top, across > 0), 4 - (across == 1).astype(jnp.int32), 0)

    @pl.when(heard > 0)
    def _():
        pl.semaphore_wait(barrier, heard)

    for (kind, index), (peer, inner) in peers.items():
        pl.when(inner)(functools.partial(signal, ready.at[0 if kind == "near" else index], peer))

    fetch_pos.wait()
    pltpu.make_async_copy(kv, kv, local_sem.at[1]).wait()
    block_rows, width = k_hbm.shape
    heads = q.shape[1] // width
    glob = pos.shape[1]
    factor = width**-0.5 * math.log2(math.e)

    row = lax.broadcasted_iota(jnp.int32, (2 * glob, block_rows), 0)
    column = lax.broadcasted_iota(jnp.int32, (2 * glob, block_rows), 1)
    wanted = jnp.zeros_like(row)
    for i in range(glob):
        wanted = jnp.where(lax.rem(row, glob) == i, pos[0, i], wanted)
    one_hot = jnp.where(column == wanted, 1.0, 0.0).astype(jnp.bfloat16)
    picked_k = dot(one_hot, kv[0], ((1,), (0,)))
    picked_v = dot(one_hot, kv[1], ((1,), (0,)))
    upper = lax.broadcasted_iota(jnp.int32, picked_k.shape, 0) < glob
    slabs[0, 0] = jnp.where(upper, picked_k, picked_v).astype(jnp.bfloat16)

    def slab_copy(e, f, semaphore, device, source=(0, 0)):
        return pltpu.make_async_remote_copy(
            slabs.at[source], slabs.at[e, f], send.at[0], semaphore,
            device_id=device, device_id_type=MESH,
        )

    directs = []

    def direct(targets):
        for h, l in targets:
            e = 2 * (hi + change(hi_signs, h)) + (1 - side if l else side)
            wanted_there = level > 0 if h < 2 and l == 0 else jnp.logical_and(top, across > 0)
            wanted_there = jnp.logical_and(wanted_there, e > 0)
            pl.when(wanted_there)(slab_copy(e, level, rest_recv, {"hi": h, "lo": l}).start)
            directs.append(wanted_there)

    direct(DIRECT[:2])

    lo_bits, hi_bits = n_lo.bit_length() - 1, n_hi.bit_length() - 1
    near_partners = [("near", 2 * 2**b) for b in range(hi_bits)] + [("near", 1)]
    far_partners = [("far", 2**b) for b in range(lo_bits - 1)]
    partners = near_partners + far_partners

    def slab_start(key):
        kind, index = key
        if kind == "near":
            slab_copy(index, 0, far_recv.at[0], near[index][0]).start()
        else:
            slab_copy(0, index, far_recv.at[index], far[index][0]).start()

    def block_start(key):
        pltpu.make_async_remote_copy(
            kv, kv_in.at[partners.index(key)], send.at[1],
            block_recv.at[0 if key in near_partners else 1],
            device_id=peers[key][0], device_id_type=MESH,
        ).start()

    inward = list(far_keys) + list(reversed(near_keys))
    for key in inward:
        pl.when(peers[key][1])(functools.partial(slab_start, key))
    direct(DIRECT[2:])
    for key in inward:
        if key in partners:
            pl.when(peers[key][1])(functools.partial(block_start, key))

    fetch_q.wait()
    stacked = jnp.concatenate([q[:, h * width : (h + 1) * width] for h in range(heads)], axis=0)
    state = attend(None, stacked, kv[0], kv[1], factor)

    def outer(key, action):
        pl.when(jnp.logical_not(peers[key][1]))(functools.partial(action, key))

    def answered(key):
        pl.semaphore_wait(ready.at[key[1]], 1)
        slab_start(key)

    outer_near = n_near - 1 - count(inner for _, inner in near.values())

    def outward_near():
        @pl.when(outer_near > 0)
        def _():
            pl.semaphore_wait(ready.at[0], outer_near)

        for key in near_keys:
            outer(key, slab_start)

    def outward_near_blocks():
        for key in near_partners:
            outer(key, block_start)

    def outward_far(slab_keys, block_keys):
        for key in slab_keys:
            outer(key, answered)
        for key in block_keys:
            if key in far_partners:
                outer(key, block_start)

    outward_far(far_keys[:1], [])
    outward_far([], far_keys[:1])
    outward_near()
    outward_near_blocks()
    outward_far(far_keys[1:2], [])
    outward_far(far_keys[2:], [])
    outward_far([], far_keys[1:])

    climb = n_far - 1 - level
    spread = {e: outward(e // 2, e % 2) for e in near}

    reach = {e: 1 if e == 2 else 0 for e in near}

    def served(e, f):
        target = near[e][0]
        flags = [
            jnp.logical_and(target["hi"] < 2, target["lo"] == 0),
            jnp.logical_and(top, spread[e] <= -reach[e]),
        ]
        if f == n_far - 1:
            edge = jnp.logical_and(level == 0, across > 0)
            flags.append(jnp.logical_and(edge, across + spread[e] <= 1))
        return functools.reduce(jnp.logical_or, flags)

    relays = {(e, f): jnp.logical_not(served(e, f)) for f in far for e in near}
    carried = {e: jnp.logical_and(jnp.logical_not(top), spread[e] >= reach[e]) for e in near}

    def relay(f):
        slab = slabs.at[0, f]
        pltpu.make_async_copy(slab, slab, far_recv.at[f]).wait()
        for e in reversed(near):
            pl.when(relays[e, f])(slab_copy(e, f, rest_recv, near[e][0], (0, f)).start)

    def raise_slabs():
        group = slabs.at[1:, 0]
        pltpu.make_async_copy(group, group, far_recv.at[0]).wait()
        for e, flag in carried.items():
            pl.when(flag)(slab_copy(e, climb, rest_recv, {"lo": lo + 2 * climb}, (e, 0)).start)

    def take(state, begin, end, semaphore):
        group = kv_in.at[begin:end]
        pltpu.make_async_copy(group, group, semaphore).wait()
        rows = (end - begin) * block_rows
        keys = kv_in[begin:end, 0].reshape(rows, width)
        values = kv_in[begin:end, 1].reshape(rows, width)
        return attend(state, stacked, keys, values, factor)

    def gather(state, begin, end):
        mixed = slabs[:, begin:end].astype(jnp.float32)
        rows = (end - begin) * n_near * glob
        keys = mixed[:, :, :glob].reshape(rows, width).astype(jnp.bfloat16)
        values = mixed[:, :, glob:].reshape(rows, width).astype(jnp.bfloat16)
        return attend(state, stacked, keys, values, factor)

    for f in range(1, n_far - 1):
        relay(f)
    raise_slabs()
    relay(n_far - 1)
    state = take(state, 0, len(near_partners), block_recv.at[0])
    state = take(state, len(near_partners), len(partners), block_recv.at[1])
    state = gather(state, 0, 1)

    pltpu.make_async_copy(kv_in, kv_in, send.at[1]).wait()
    sent = n_near + n_far - 2 + count([*directs, *relays.values(), *carried.values()])
    amount = 1
    while amount <= total:
        part = slabs.at[0, :amount] if amount <= n_far else slabs.at[: amount // n_far]
        pl.when(lax.rem(lax.div(sent, amount), 2) == 1)(pltpu.make_async_copy(part, part, send.at[0]).wait)
        amount *= 2

    rest = slabs.at[1:, 1:]
    pltpu.make_async_copy(rest, rest, rest_recv).wait()
    _, denominator, numerator = gather(state, 1, n_far)
    result = numerator * (1.0 / denominator)
    for h in range(heads):
        part = result[:, h * block_rows : (h + 1) * block_rows]
        out_ref[:, h * width : (h + 1) * width] = jnp.transpose(part).astype(out_ref.dtype)


def local(n_hi, n_lo, queries, key_rows, value_rows, global_positions):
    partners = (n_lo.bit_length() - 1) + (n_hi.bit_length() - 1)
    glob = global_positions.shape[1]
    width = key_rows.shape[1]
    dma = pltpu.SemaphoreType.DMA
    return pl.pallas_call(
        functools.partial(kernel, n_hi, n_lo),
        out_shape=jax.ShapeDtypeStruct(queries.shape, queries.dtype),
        in_specs=[pl.BlockSpec(memory_space=pltpu.HBM)] * 4,
        out_specs=pl.BlockSpec(memory_space=pltpu.VMEM),
        scratch_shapes=[
            pltpu.VMEM(queries.shape, queries.dtype),
            pltpu.VMEM((2,) + key_rows.shape, key_rows.dtype),
            pltpu.SMEM(global_positions.shape, global_positions.dtype),
            pltpu.VMEM((2 * n_hi, n_lo // 2, 2 * glob, width), key_rows.dtype),
            pltpu.VMEM((partners, 2) + key_rows.shape, key_rows.dtype),
            dma((3,)),
            pltpu.SemaphoreType.REGULAR((n_lo // 2,)),
            dma((n_lo // 2,)),
            dma,
            dma((2,)),
            dma((2,)),
        ],
        compiler_params=pltpu.CompilerParams(collective_id=0, has_side_effects=True, vmem_limit_bytes=12 * 2**20),
    )(*(pltpu.with_memory_space_constraint(x, pltpu.HBM) for x in (queries, key_rows, value_rows, global_positions)))


def solution(mesh):
    spec = P(("hi", "lo"), None)
    return jax.shard_map(
        functools.partial(local, mesh.shape["hi"], mesh.shape["lo"]),
        mesh=mesh,
        in_specs=(spec,) * 4,
        out_specs=spec,
        check_vma=False,
    )
```

```python
import functools
import math

import jax
import jax.numpy as jnp
from jax import lax
from jax.experimental import pallas as pl
from jax.experimental.pallas import tpu as pltpu
from jax.sharding import PartitionSpec as P

MESH = pl.DeviceIdType.MESH
DIRECT = [(0, 0), (1, 0), (0, 1), (1, 1), (2, 0), (3, 0)]


def dot(a, b, dims):
    return lax.dot_general(a, b, (dims, ((), ())), preferred_element_type=jnp.float32)


def attend(state, stacked, keys, values, factor):
    scores = dot(keys, stacked, ((1,), (1,)))
    fresh = jnp.max(scores, axis=0, keepdims=True)
    if state is not None:
        running, denominator, numerator = state
        fresh = jnp.maximum(running, fresh)
    weights = jnp.exp2((scores - fresh) * factor)
    total = jnp.sum(weights, axis=0, keepdims=True)
    update = dot(values, weights.astype(jnp.bfloat16), ((0,), (0,)))
    if state is not None:
        fade = jnp.exp2((running - fresh) * factor)
        total = denominator * fade + total
        update = numerator * fade + update
    return fresh, total, update


def turns(index, size):
    bits = (2**b for b in range(size.bit_length() - 1))
    return [1 - 2 * lax.rem(lax.div(index, bit), 2) for bit in bits]


def change(signs, mask, weight=lambda b: 2**b):
    parts = [sign * weight(b) for b, sign in enumerate(signs) if mask & 2**b and weight(b)]
    return sum(parts[1:], parts[0]) if parts else 0


def count(flags):
    return sum(flag.astype(jnp.int32) for flag in flags)


def kernel(
    n_hi, n_lo, q_hbm, k_hbm, v_hbm, pos_hbm, out_ref,
    q, kv, pos, slabs, kv_in, local_sem, ready, far_recv, rest_recv, send, block_recv,
):
    fetch_pos = pltpu.make_async_copy(pos_hbm, pos, local_sem.at[0])
    fetch_q = pltpu.make_async_copy(q_hbm, q, local_sem.at[2])
    fetch_pos.start()
    pltpu.make_async_copy(k_hbm, kv.at[0], local_sem.at[1]).start()
    pltpu.make_async_copy(v_hbm, kv.at[1], local_sem.at[1]).start()
    fetch_q.start()

    hi, lo = lax.axis_index("hi"), lax.axis_index("lo")
    barrier = pltpu.get_barrier_semaphore()
    n_far, n_near, total = n_lo // 2, n_hi * 2, n_hi * n_lo
    level, side = lax.div(lo, 2), lax.rem(lo, 2)
    across = lax.div(hi, 2) + side
    top = level == n_far - 1
    hi_signs, lo_signs = turns(hi, n_hi), turns(lo, n_lo)

    def outward(mask_hi, mask_lo):
        return change(hi_signs, mask_hi, lambda b: 2**b // 2) + change(lo_signs, mask_lo, lambda b: max(1, 2**b // 2))

    def peer_of(f, e):
        mask_hi, mask_lo = e // 2, 2 * f + e % 2
        up, along = change(hi_signs, mask_hi), change(lo_signs, mask_lo)
        inner = outward(mask_hi, mask_lo) * total + up * n_lo + along < 0
        return {"hi": hi + up, "lo": lo + along}, inner

    near = {e: peer_of(0, e) for e in range(1, n_near)}
    far = {f: peer_of(f, 0) for f in range(1, n_far)}
    peers = {("near", e): p for e, p in near.items()} | {("far", f): p for f, p in far.items()}
    near_keys, far_keys = [("near", e) for e in near], [("far", f) for f in far]

    def signal(semaphore, device):
        pl.semaphore_signal(semaphore, inc=1, device_id=device, device_id_type=MESH)

    @pl.when(jnp.logical_and(level == 0, across == 1))
    def _():
        for h in range(n_hi):
            for y in range(2):
                if h > 1 or y:
                    flag = jnp.logical_or(h != hi, y != side)
                    pl.when(flag)(functools.partial(signal, barrier, {"hi": h, "lo": n_lo - 2 + y}))

    for peer, inner in peers.values():
        pl.when(jnp.logical_not(inner))(functools.partial(signal, barrier, peer))

    @pl.when(jnp.logical_and(level == 0, across == 0))
    def _():
        def greet(l, carry):
            for h in range(n_hi):
                pl.when(jnp.logical_or(h != hi, lax.rem(l, 2) == 1))(functools.partial(signal, barrier, {"hi": h, "lo": l}))
            return carry

        lax.fori_loop(2, n_lo, greet, 0)

    heard = count(inner for _, inner in peers.values())
    heard = heard + jnp.where(level > 0, 2 - (across == 0).astype(jnp.int32), 0)
    heard = heard + jnp.where(jnp.logical_and(top, across > 0), 4 - (across == 1).astype(jnp.int32), 0)

    @pl.when(heard > 0)
    def _():
        pl.semaphore_wait(barrier, heard)

    for (kind, index), (peer, inner) in peers.items():
        pl.when(inner)(functools.partial(signal, ready.at[0 if kind == "near" else index], peer))

    fetch_pos.wait()
    pltpu.make_async_copy(kv, kv, local_sem.at[1]).wait()
    block_rows, width = k_hbm.shape
    heads = q.shape[1] // width
    glob = pos.shape[1]
    factor = width**-0.5 * math.log2(math.e)

    row = lax.broadcasted_iota(jnp.int32, (2 * glob, block_rows), 0)
    column = lax.broadcasted_iota(jnp.int32, (2 * glob, block_rows), 1)
    wanted = jnp.zeros_like(row)
    for i in range(glob):
        wanted = jnp.where(lax.rem(row, glob) == i, pos[0, i], wanted)
    one_hot = jnp.where(column == wanted, 1.0, 0.0).astype(jnp.bfloat16)
    picked_k = dot(one_hot, kv[0], ((1,), (0,)))
    picked_v = dot(one_hot, kv[1], ((1,), (0,)))
    upper = lax.broadcasted_iota(jnp.int32, picked_k.shape, 0) < glob
    slabs[0, 0] = jnp.where(upper, picked_k, picked_v).astype(jnp.bfloat16)

    def slab_copy(e, f, semaphore, device, source=(0, 0)):
        return pltpu.make_async_remote_copy(
            slabs.at[source], slabs.at[e, f], send, semaphore,
            device_id=device, device_id_type=MESH,
        )

    directs = []

    def direct(targets):
        for h, l in targets:
            e = 2 * (hi + change(hi_signs, h)) + (1 - side if l else side)
            wanted_there = level > 0 if h < 2 and l == 0 else jnp.logical_and(top, across > 0)
            wanted_there = jnp.logical_and(wanted_there, e > 0)
            pl.when(wanted_there)(slab_copy(e, level, rest_recv, {"hi": h, "lo": l}).start)
            directs.append(wanted_there)

    direct(DIRECT[:2])

    lo_bits, hi_bits = n_lo.bit_length() - 1, n_hi.bit_length() - 1
    near_partners = [("near", 2 * 2**b) for b in range(hi_bits)] + [("near", 1)]
    far_partners = [("far", 2**b) for b in range(lo_bits - 1)]
    partners = near_partners + far_partners

    def slab_start(key):
        kind, index = key
        if kind == "near":
            slab_copy(index, 0, far_recv.at[0], near[index][0]).start()
        else:
            slab_copy(0, index, far_recv.at[index], far[index][0]).start()

    def block_start(key):
        pltpu.make_async_remote_copy(
            kv, kv_in.at[partners.index(key)], send,
            block_recv.at[0 if key in near_partners else 1],
            device_id=peers[key][0], device_id_type=MESH,
        ).start()

    inward = list(far_keys) + list(reversed(near_keys))
    for key in inward:
        pl.when(peers[key][1])(functools.partial(slab_start, key))
    direct(DIRECT[2:])
    for key in inward:
        if key in partners:
            pl.when(peers[key][1])(functools.partial(block_start, key))

    fetch_q.wait()
    stacked = jnp.concatenate([q[:, h * width : (h + 1) * width] for h in range(heads)], axis=0)
    state = attend(None, stacked, kv[0], kv[1], factor)

    def outer(key, action):
        pl.when(jnp.logical_not(peers[key][1]))(functools.partial(action, key))

    def answered(key):
        pl.semaphore_wait(ready.at[key[1]], 1)
        slab_start(key)

    outer_near = n_near - 1 - count(inner for _, inner in near.values())

    def outward_near():
        @pl.when(outer_near > 0)
        def _():
            pl.semaphore_wait(ready.at[0], outer_near)

        for key in near_keys:
            outer(key, slab_start)

    def outward_near_blocks():
        for key in near_partners:
            outer(key, block_start)

    def outward_far(slab_keys, block_keys):
        for key in slab_keys:
            outer(key, answered)
        for key in block_keys:
            if key in far_partners:
                outer(key, block_start)

    outward_far(far_keys[:1], [])
    outward_far([], far_keys[:1])
    outward_near()
    outward_near_blocks()
    outward_far(far_keys[1:2], [])
    outward_far(far_keys[2:], [])
    outward_far([], far_keys[1:])

    climb = n_far - 1 - level
    spread = {e: outward(e // 2, e % 2) for e in near}

    reach = {e: 1 if e == 2 else 0 for e in near}

    def served(e, f):
        target = near[e][0]
        flags = [
            jnp.logical_and(target["hi"] < 2, target["lo"] == 0),
            jnp.logical_and(top, spread[e] <= -reach[e]),
        ]
        if f == n_far - 1:
            edge = jnp.logical_and(level == 0, across > 0)
            flags.append(jnp.logical_and(edge, across + spread[e] <= 1))
        return functools.reduce(jnp.logical_or, flags)

    relays = {(e, f): jnp.logical_not(served(e, f)) for f in far for e in near}
    carried = {e: jnp.logical_and(jnp.logical_not(top), spread[e] >= reach[e]) for e in near}

    def relay(f):
        slab = slabs.at[0, f]
        pltpu.make_async_copy(slab, slab, far_recv.at[f]).wait()
        for e in reversed(near):
            pl.when(relays[e, f])(slab_copy(e, f, rest_recv, near[e][0], (0, f)).start)

    def raise_slabs():
        group = slabs.at[1:, 0]
        pltpu.make_async_copy(group, group, far_recv.at[0]).wait()
        for e, flag in carried.items():
            pl.when(flag)(slab_copy(e, climb, rest_recv, {"lo": lo + 2 * climb}, (e, 0)).start)

    def take(state, begin, end, semaphore):
        group = kv_in.at[begin:end]
        pltpu.make_async_copy(group, group, semaphore).wait()
        rows = (end - begin) * block_rows
        keys = kv_in[begin:end, 0].reshape(rows, width)
        values = kv_in[begin:end, 1].reshape(rows, width)
        return attend(state, stacked, keys, values, factor)

    def gather(state, begin, end):
        mixed = slabs[:, begin:end].astype(jnp.float32)
        rows = (end - begin) * n_near * glob
        keys = mixed[:, :, :glob].reshape(rows, width).astype(jnp.bfloat16)
        values = mixed[:, :, glob:].reshape(rows, width).astype(jnp.bfloat16)
        return attend(state, stacked, keys, values, factor)

    for f in range(1, n_far - 1):
        relay(f)
    raise_slabs()
    relay(n_far - 1)
    state = take(state, 0, len(near_partners), block_recv.at[0])
    state = take(state, len(near_partners), len(partners), block_recv.at[1])
    state = gather(state, 0, 1)

    pltpu.make_async_copy(kv_in, kv_in, send).wait()
    sent = n_near + n_far - 2 + count([*directs, *relays.values(), *carried.values()])
    amount = 1
    while amount <= total:
        part = slabs.at[0, :amount] if amount <= n_far else slabs.at[: amount // n_far]
        pl.when(lax.rem(lax.div(sent, amount), 2) == 1)(pltpu.make_async_copy(part, part, send).wait)
        amount *= 2

    rest = slabs.at[1:, 1:]
    pltpu.make_async_copy(rest, rest, rest_recv).wait()
    _, denominator, numerator = gather(state, 1, n_far)
    result = numerator * (1.0 / denominator)
    for h in range(heads):
        part = result[:, h * block_rows : (h + 1) * block_rows]
        out_ref[:, h * width : (h + 1) * width] = jnp.transpose(part.astype(out_ref.dtype))


def local(n_hi, n_lo, queries, key_rows, value_rows, global_positions):
    partners = (n_lo.bit_length() - 1) + (n_hi.bit_length() - 1)
    glob = global_positions.shape[1]
    width = key_rows.shape[1]
    dma = pltpu.SemaphoreType.DMA
    return pl.pallas_call(
        functools.partial(kernel, n_hi, n_lo),
        out_shape=jax.ShapeDtypeStruct(queries.shape, queries.dtype),
        in_specs=[pl.BlockSpec(memory_space=pltpu.HBM)] * 4,
        out_specs=pl.BlockSpec(memory_space=pltpu.VMEM),
        scratch_shapes=[
            pltpu.VMEM(queries.shape, queries.dtype),
            pltpu.VMEM((2,) + key_rows.shape, key_rows.dtype),
            pltpu.SMEM(global_positions.shape, global_positions.dtype),
            pltpu.VMEM((2 * n_hi, n_lo // 2, 2 * glob, width), key_rows.dtype),
            pltpu.VMEM((partners, 2) + key_rows.shape, key_rows.dtype),
            dma((3,)),
            pltpu.SemaphoreType.REGULAR((n_lo // 2,)),
            dma((n_lo // 2,)),
            dma,
            dma,
            dma((2,)),
        ],
        compiler_params=pltpu.CompilerParams(collective_id=0, has_side_effects=True, vmem_limit_bytes=12 * 2**20),
    )(*(pltpu.with_memory_space_constraint(x, pltpu.HBM) for x in (queries, key_rows, value_rows, global_positions)))


def solution(mesh):
    spec = P(("hi", "lo"), None)
    return jax.shard_map(
        functools.partial(local, mesh.shape["hi"], mesh.shape["lo"]),
        mesh=mesh,
        in_specs=(spec,) * 4,
        out_specs=spec,
        check_vma=False,
    )
```

```python
import functools
import math

import jax
import jax.numpy as jnp
from jax import lax
from jax.experimental import pallas as pl
from jax.experimental.pallas import tpu as pltpu
from jax.sharding import PartitionSpec as P

MESH = pl.DeviceIdType.MESH
DIRECT = [(0, 0), (1, 0), (0, 1), (1, 1), (2, 0), (3, 0)]


def dot(a, b, dims):
    return lax.dot_general(a, b, (dims, ((), ())), preferred_element_type=jnp.float32)


def attend(state, stacked, keys, values, factor):
    scores = dot(keys, stacked, ((1,), (1,)))
    fresh = jnp.max(scores, axis=0, keepdims=True)
    if state is not None:
        running, denominator, numerator = state
        fresh = jnp.maximum(running, fresh)
    weights = jnp.exp2((scores - fresh) * factor)
    total = jnp.sum(weights, axis=0, keepdims=True)
    update = dot(values, weights.astype(jnp.bfloat16), ((0,), (0,)))
    if state is not None:
        fade = jnp.exp2((running - fresh) * factor)
        total = denominator * fade + total
        update = numerator * fade + update
    return fresh, total, update


def turns(index, size):
    bits = (2**b for b in range(size.bit_length() - 1))
    return [1 - 2 * lax.rem(lax.div(index, bit), 2) for bit in bits]


def change(signs, mask, weight=lambda b: 2**b):
    parts = [sign * weight(b) for b, sign in enumerate(signs) if mask & 2**b and weight(b)]
    return sum(parts[1:], parts[0]) if parts else 0


def count(flags):
    return sum(flag.astype(jnp.int32) for flag in flags)


def kernel(
    n_hi, n_lo, q_hbm, k_hbm, v_hbm, pos_hbm, out_ref,
    q, kv, pos, slabs, kv_in, local_sem, ready, far_recv, rest_recv, send, block_recv,
):
    fetch_pos = pltpu.make_async_copy(pos_hbm, pos, local_sem.at[0])
    fetch_q = pltpu.make_async_copy(q_hbm, q, local_sem.at[2])
    fetch_pos.start()
    pltpu.make_async_copy(k_hbm, kv.at[0], local_sem.at[1]).start()
    pltpu.make_async_copy(v_hbm, kv.at[1], local_sem.at[1]).start()
    fetch_q.start()

    hi, lo = lax.axis_index("hi"), lax.axis_index("lo")
    barrier = pltpu.get_barrier_semaphore()
    n_far, n_near, total = n_lo // 2, n_hi * 2, n_hi * n_lo
    level, side = lax.div(lo, 2), lax.rem(lo, 2)
    across = lax.div(hi, 2) + side
    top = level == n_far - 1
    hi_signs, lo_signs = turns(hi, n_hi), turns(lo, n_lo)

    def outward(mask_hi, mask_lo):
        return change(hi_signs, mask_hi, lambda b: 2**b // 2) + change(lo_signs, mask_lo, lambda b: max(1, 2**b // 2))

    def peer_of(f, e):
        mask_hi, mask_lo = e // 2, 2 * f + e % 2
        up, along = change(hi_signs, mask_hi), change(lo_signs, mask_lo)
        inner = outward(mask_hi, mask_lo) * total + up * n_lo + along < 0
        return {"hi": hi + up, "lo": lo + along}, inner

    near = {e: peer_of(0, e) for e in range(1, n_near)}
    far = {f: peer_of(f, 0) for f in range(1, n_far)}
    peers = {("near", e): p for e, p in near.items()} | {("far", f): p for f, p in far.items()}
    near_keys, far_keys = [("near", e) for e in near], [("far", f) for f in far]

    def signal(semaphore, device):
        pl.semaphore_signal(semaphore, inc=1, device_id=device, device_id_type=MESH)

    @pl.when(jnp.logical_and(level == 0, across == 1))
    def _():
        for h in range(n_hi):
            for y in range(2):
                if h > 1 or y:
                    flag = jnp.logical_or(h != hi, y != side)
                    pl.when(flag)(functools.partial(signal, barrier, {"hi": h, "lo": n_lo - 2 + y}))

    for peer, inner in peers.values():
        pl.when(jnp.logical_not(inner))(functools.partial(signal, barrier, peer))

    @pl.when(jnp.logical_and(level == 0, across == 0))
    def _():
        def greet(l, carry):
            for h in range(n_hi):
                pl.when(jnp.logical_or(h != hi, lax.rem(l, 2) == 1))(functools.partial(signal, barrier, {"hi": h, "lo": l}))
            return carry

        lax.fori_loop(2, n_lo, greet, 0)

    heard = count(inner for _, inner in peers.values())
    heard = heard + jnp.where(level > 0, 2 - (across == 0).astype(jnp.int32), 0)
    heard = heard + jnp.where(jnp.logical_and(top, across > 0), 4 - (across == 1).astype(jnp.int32), 0)

    @pl.when(heard > 0)
    def _():
        pl.semaphore_wait(barrier, heard)

    for (kind, index), (peer, inner) in peers.items():
        pl.when(inner)(functools.partial(signal, ready.at[0 if kind == "near" else index], peer))

    fetch_pos.wait()
    pltpu.make_async_copy(kv, kv, local_sem.at[1]).wait()
    block_rows, width = k_hbm.shape
    heads = q.shape[1] // width
    glob = pos.shape[1]
    factor = width**-0.5 * math.log2(math.e)

    row = lax.broadcasted_iota(jnp.int32, (2 * glob, block_rows), 0)
    column = lax.broadcasted_iota(jnp.int32, (2 * glob, block_rows), 1)
    wanted = jnp.zeros_like(row)
    for i in range(glob):
        wanted = jnp.where(lax.rem(row, glob) == i, pos[0, i], wanted)
    one_hot = jnp.where(column == wanted, 1.0, 0.0).astype(jnp.bfloat16)
    picked_k = dot(one_hot, kv[0], ((1,), (0,)))
    picked_v = dot(one_hot, kv[1], ((1,), (0,)))
    upper = lax.broadcasted_iota(jnp.int32, picked_k.shape, 0) < glob
    slabs[0, 0] = jnp.where(upper, picked_k, picked_v).astype(jnp.bfloat16)

    def slab_copy(e, f, semaphore, device, source=(0, 0)):
        return pltpu.make_async_remote_copy(
            slabs.at[source], slabs.at[e, f], send, semaphore,
            device_id=device, device_id_type=MESH,
        )

    directs = []

    def direct(targets):
        for h, l in targets:
            e = 2 * (hi + change(hi_signs, h)) + (1 - side if l else side)
            wanted_there = level > 0 if h < 2 and l == 0 else jnp.logical_and(top, across > 0)
            wanted_there = jnp.logical_and(wanted_there, e > 0)
            pl.when(wanted_there)(slab_copy(e, level, rest_recv.at[jnp.clip(level, 1, 2) - 1], {"hi": h, "lo": l}).start)
            directs.append(wanted_there)

    direct(DIRECT[:2])

    lo_bits, hi_bits = n_lo.bit_length() - 1, n_hi.bit_length() - 1
    near_partners = [("near", 2 * 2**b) for b in range(hi_bits)] + [("near", 1)]
    far_partners = [("far", 2**b) for b in range(lo_bits - 1)]
    partners = near_partners + far_partners

    def slab_start(key):
        kind, index = key
        if kind == "near":
            slab_copy(index, 0, far_recv.at[0], near[index][0]).start()
        else:
            slab_copy(0, index, far_recv.at[index], far[index][0]).start()

    def block_start(key):
        pltpu.make_async_remote_copy(
            kv, kv_in.at[partners.index(key)], send,
            block_recv.at[0 if key in near_partners else 1],
            device_id=peers[key][0], device_id_type=MESH,
        ).start()

    inward = list(far_keys) + list(reversed(near_keys))
    for key in inward:
        pl.when(peers[key][1])(functools.partial(slab_start, key))
    direct(DIRECT[2:])
    for key in inward:
        if key in partners:
            pl.when(peers[key][1])(functools.partial(block_start, key))

    fetch_q.wait()
    stacked = jnp.concatenate([q[:, h * width : (h + 1) * width] for h in range(heads)], axis=0)
    state = attend(None, stacked, kv[0], kv[1], factor)

    def outer(key, action):
        pl.when(jnp.logical_not(peers[key][1]))(functools.partial(action, key))

    def answered(key):
        pl.semaphore_wait(ready.at[key[1]], 1)
        slab_start(key)

    outer_near = n_near - 1 - count(inner for _, inner in near.values())

    def outward_near():
        @pl.when(outer_near > 0)
        def _():
            pl.semaphore_wait(ready.at[0], outer_near)

        for key in near_keys:
            outer(key, slab_start)

    def outward_near_blocks():
        for key in near_partners:
            outer(key, block_start)

    def outward_far(slab_keys, block_keys):
        for key in slab_keys:
            outer(key, answered)
        for key in block_keys:
            if key in far_partners:
                outer(key, block_start)

    outward_far(far_keys[:1], [])
    outward_far([], far_keys[:1])
    outward_near()
    outward_near_blocks()
    outward_far(far_keys[1:2], [])
    outward_far(far_keys[2:], [])
    outward_far([], far_keys[1:])

    climb = n_far - 1 - level
    spread = {e: outward(e // 2, e % 2) for e in near}

    reach = {e: 1 if e == 2 else 0 for e in near}

    def served(e, f):
        target = near[e][0]
        flags = [
            jnp.logical_and(target["hi"] < 2, target["lo"] == 0),
            jnp.logical_and(top, spread[e] <= -reach[e]),
        ]
        if f == n_far - 1:
            edge = jnp.logical_and(level == 0, across > 0)
            flags.append(jnp.logical_and(edge, across + spread[e] <= 1))
        return functools.reduce(jnp.logical_or, flags)

    relays = {(e, f): jnp.logical_not(served(e, f)) for f in far for e in near}
    carried = {e: jnp.logical_and(jnp.logical_not(top), spread[e] >= reach[e]) for e in near}

    def relay(f):
        slab = slabs.at[0, f]
        pltpu.make_async_copy(slab, slab, far_recv.at[f]).wait()
        for e in reversed(near):
            pl.when(relays[e, f])(slab_copy(e, f, rest_recv.at[min(f, 2) - 1], near[e][0], (0, f)).start)

    def raise_slabs():
        group = slabs.at[1:, 0]
        pltpu.make_async_copy(group, group, far_recv.at[0]).wait()
        for e, flag in carried.items():
            pl.when(flag)(slab_copy(e, climb, rest_recv.at[jnp.minimum(climb, 2) - 1], {"lo": lo + 2 * climb}, (e, 0)).start)

    def take(state, begin, end, semaphore):
        group = kv_in.at[begin:end]
        pltpu.make_async_copy(group, group, semaphore).wait()
        rows = (end - begin) * block_rows
        keys = kv_in[begin:end, 0].reshape(rows, width)
        values = kv_in[begin:end, 1].reshape(rows, width)
        return attend(state, stacked, keys, values, factor)

    def gather(state, begin, end):
        mixed = slabs[:, begin:end].astype(jnp.float32)
        rows = (end - begin) * n_near * glob
        keys = mixed[:, :, :glob].reshape(rows, width).astype(jnp.bfloat16)
        values = mixed[:, :, glob:].reshape(rows, width).astype(jnp.bfloat16)
        return attend(state, stacked, keys, values, factor)

    for f in range(1, n_far - 1):
        relay(f)
    raise_slabs()
    relay(n_far - 1)
    state = take(state, 0, len(near_partners), block_recv.at[0])
    state = take(state, len(near_partners), len(partners), block_recv.at[1])
    early = slabs.at[1:, 1]
    pltpu.make_async_copy(early, early, rest_recv.at[0]).wait()
    state = gather(state, 0, 2)

    pltpu.make_async_copy(kv_in, kv_in, send).wait()
    sent = n_near + n_far - 2 + count([*directs, *relays.values(), *carried.values()])
    amount = 1
    while amount <= total:
        part = slabs.at[0, :amount] if amount <= n_far else slabs.at[: amount // n_far]
        pl.when(lax.rem(lax.div(sent, amount), 2) == 1)(pltpu.make_async_copy(part, part, send).wait)
        amount *= 2

    rest = slabs.at[1:, 2:]
    pltpu.make_async_copy(rest, rest, rest_recv.at[1]).wait()
    _, denominator, numerator = gather(state, 2, n_far)
    result = numerator * (1.0 / denominator)
    for h in range(heads):
        part = result[:, h * block_rows : (h + 1) * block_rows]
        out_ref[:, h * width : (h + 1) * width] = jnp.transpose(part.astype(out_ref.dtype))


def local(n_hi, n_lo, queries, key_rows, value_rows, global_positions):
    partners = (n_lo.bit_length() - 1) + (n_hi.bit_length() - 1)
    glob = global_positions.shape[1]
    width = key_rows.shape[1]
    dma = pltpu.SemaphoreType.DMA
    return pl.pallas_call(
        functools.partial(kernel, n_hi, n_lo),
        out_shape=jax.ShapeDtypeStruct(queries.shape, queries.dtype),
        in_specs=[pl.BlockSpec(memory_space=pltpu.HBM)] * 4,
        out_specs=pl.BlockSpec(memory_space=pltpu.VMEM),
        scratch_shapes=[
            pltpu.VMEM(queries.shape, queries.dtype),
            pltpu.VMEM((2,) + key_rows.shape, key_rows.dtype),
            pltpu.SMEM(global_positions.shape, global_positions.dtype),
            pltpu.VMEM((2 * n_hi, n_lo // 2, 2 * glob, width), key_rows.dtype),
            pltpu.VMEM((partners, 2) + key_rows.shape, key_rows.dtype),
            dma((3,)),
            pltpu.SemaphoreType.REGULAR((n_lo // 2,)),
            dma((n_lo // 2,)),
            dma((2,)),
            dma,
            dma((2,)),
        ],
        compiler_params=pltpu.CompilerParams(collective_id=0, has_side_effects=True, vmem_limit_bytes=12 * 2**20),
    )(*(pltpu.with_memory_space_constraint(x, pltpu.HBM) for x in (queries, key_rows, value_rows, global_positions)))


def solution(mesh):
    spec = P(("hi", "lo"), None)
    return jax.shard_map(
        functools.partial(local, mesh.shape["hi"], mesh.shape["lo"]),
        mesh=mesh,
        in_specs=(spec,) * 4,
        out_specs=spec,
        check_vma=False,
    )
```
